128 devices in a mesh: dp: 32 (over x, z, core), tensor: 4 (over y).
Axes of the slice: x: 4, y: 4, z: 4, core: 2. Of those that a mesh axis runs over, the one named last changes fastest.
Arguments:
- hidden_in: bfloat16 [32768, 768], P('dp'), may hold values from -6 to 6
- segments: int32 [32768], P('dp'), may hold values from 0 to 63, as said below
- positions: int32 [32768], P('dp'), may hold values from 0 to 1023, as said below
- first_gain: float32 [768], replicated, may hold values from 0.1 to 1.9
- first_shift: float32 [768], replicated, may hold values from -2 to 2
- heads_weight: bfloat16 [768, 2304], P(None, 'tensor'), may hold values from -0.21875 to 0.21875
- heads_bias: float32 [2304], P('tensor'), may hold values from -2 to 2
- dense_weight: bfloat16 [768, 768], P('tensor'), may hold values from -0.875 to 0.875
- dense_bias: float32 [768], replicated, may hold values from -3 to 3
- second_gain: float32 [768], replicated, may hold values from 0.1 to 1.9
- second_shift: float32 [768], replicated, may hold values from -2 to 2
- expand_weight: bfloat16 [768, 3072], P(None, 'tensor'), may hold values from -0.21875 to 0.21875
- expand_bias: float32 [3072], P('tensor'), may hold values from -3 to 3
- shrink_weight: bfloat16 [3072, 768], P('tensor'), may hold values from -0.109375 to 0.109375
- shrink_bias: float32 [768], replicated, may hold values from -3 to 3
- cotangent: bfloat16 [32768, 768], P('dp'), may hold values from -6 to 6
Outputs:
- hidden_out: bfloat16 [32768, 768], P('dp')
- hidden_gradient: bfloat16 [32768, 768], P('dp')
- first_gain_gradient: float32 [768], replicated
- first_shift_gradient: float32 [768], replicated
- heads_weight_gradient: float32 [768, 2304], P(None, 'tensor')
- heads_bias_gradient: float32 [2304], P('tensor')
- dense_weight_gradient: float32 [768, 768], P('tensor')
- dense_bias_gradient: float32 [768], replicated
- second_gain_gradient: float32 [768], replicated
- second_shift_gradient: float32 [768], replicated
- expand_weight_gradient: float32 [768, 3072], P(None, 'tensor')
- expand_bias_gradient: float32 [3072], P('tensor')
- shrink_weight_gradient: float32 [3072, 768], P('tensor')
- shrink_bias_gradient: float32 [768], replicated
The draws below stay inside these ranges and needn't reach their ends.
Inputs may be any that keep to these rules, and one draw needn't show every extreme that they name: `segments`: each sequence s of 1024 tokens (rows s * 1024 to s * 1024 + 1023) holds 2 documents numbered s * 2 to s * 2 + 1 in order, segment numbers never falling; each document has 1024 // 2 - 2 * (128) tokens or more. Within a document positions rise by one from token to token; the first document of each sequence starts at 0; the last document of the first sequence ends at the largest position.
All inputs are finite; a program needn't handle non-finite values.
Results may differ from the reference program's by a relative error of at most 0.012.
The reference program's roundings to bfloat16 on the way count: a program that leaves them out, or rounds other values in their place, can miss the bound.
Values sent between devices are 32-bit elements; how exact they have to be, the bound alone decides.
No kernel may reach another device: no remote copies, remote signals or barrier semaphores. Data moves between devices by JAX's collectives and lax.ppermute only.
A program may use at most 128 MiB of HBM per device.

```python
import math
import jax
import jax.numpy as jnp
from jax import lax

D = 768
HD = 64
FF = 3072
LEN = 1024
ROT = 16
DOCS = 2
TOKENS = 32768
N_TENSOR = 4


def document_layout(key):
    seq_total = TOKENS // LEN
    cut_key, offset_key = jax.random.split(jax.random.fold_in(key, 17))
    jitter_reach = LEN // (4 * DOCS)
    jitter = jax.random.randint(cut_key, (seq_total, DOCS - 1), -jitter_reach, jitter_reach + 1)
    bounds = (jnp.arange(1, DOCS, dtype=jnp.int32) * (LEN // DOCS))[None, :] + jitter
    token_index = jnp.arange(LEN, dtype=jnp.int32)
    doc_local = jnp.sum((token_index[None, :, None] >= bounds[:, None, :]).astype(jnp.int32), axis=2)
    starts = jnp.concatenate([jnp.zeros((seq_total, 1), jnp.int32), bounds], axis=1)
    ends = jnp.concatenate([bounds, jnp.full((seq_total, 1), LEN, jnp.int32)], axis=1)
    doc_sizes = ends - starts
    offsets = jax.random.randint(offset_key, (seq_total, DOCS), 0, 1025 - doc_sizes)
    offsets = offsets * (jnp.arange(DOCS) > 0).astype(jnp.int32)[None, :]
    offsets = offsets.at[0, DOCS - 1].set(1024 - doc_sizes[0, DOCS - 1])
    doc_begin = jnp.take_along_axis(starts, doc_local, axis=1)
    doc_offset = jnp.take_along_axis(offsets, doc_local, axis=1)
    seg_ids = doc_local + (jnp.arange(seq_total, dtype=jnp.int32) * DOCS)[:, None]
    pos_ids = token_index[None, :] - doc_begin + doc_offset
    return (seg_ids.reshape(TOKENS).astype(jnp.int32), pos_ids.reshape(TOKENS).astype(jnp.int32))


def draw_segments(key, part):
    return document_layout(key)[0]


def draw_positions(key, part):
    return document_layout(key)[1]


def strengthened(values, rng, source, target, blocks, factor):
    def block_of(dim):
        return (jnp.arange(values.shape[dim]) // (values.shape[dim] // blocks)).reshape((-1,) + (1,) * (values.ndim - 1 - dim))

    one_side = jax.random.permutation(rng, blocks)[block_of(target)]
    far = (block_of(target) + blocks // 2) % blocks
    return jnp.where((block_of(source) == one_side) | (block_of(source) == far), factor * values, values)


def block_levels(key, dims, shards, low, top_value):
    loudness, own = 1.0, jax.random.fold_in(key, 6)
    for dim, shards_of in shards:
        draws = jnp.exp(jax.random.uniform(jax.random.fold_in(own, dim), (shards_of,), jnp.float32, low / len(shards), top_value / len(shards)))
        loudness = loudness * jnp.repeat(draws, dims[dim] // shards_of).reshape([-1 if axis == dim else 1 for axis in range(len(dims))])
    return loudness


def bell_draw(key, shape, scale, limit, cuts=(), kind=jnp.bfloat16):
    values = scale * jax.random.normal(key, shape, jnp.float32)
    if cuts:
        values = values * block_levels(key, shape, cuts, -0.22, 0.18)
    return jnp.clip(values, -limit, limit).astype(kind)


def noise_with(own_key, shape, width, limit, cuts, heavy, held_as=jnp.bfloat16):
    drawn = width * jax.random.normal(own_key, shape, jnp.float32)
    if cuts:
        drawn = drawn * block_levels(own_key, shape, cuts, -0.22, 0.18)
    return jnp.clip(strengthened(drawn, jax.random.fold_in(own_key, 3), *heavy), -limit, limit).astype(held_as)


def setup_inputs(seed: int = 0) -> dict:
    arg_keys = jax.random.split(jax.random.key(seed), 17)
    return {
        "hidden_in": noise_with(arg_keys[0], (TOKENS, D), 1.0, 6.0, ((0, 32),), (0, 1, 32, 2.75)),
        "segments": draw_segments(jax.random.fold_in(arg_keys[16], 71), 0),
        "positions": draw_positions(jax.random.fold_in(arg_keys[16], 71), 0),
        "first_gain": jnp.clip(1.0 + 0.18 * jax.random.normal(arg_keys[3], (D,), jnp.float32), 0.1, 1.9),
        "first_shift": bell_draw(arg_keys[4], (D,), 0.3, 2.0, (), jnp.float32),
        "heads_weight": bell_draw(arg_keys[5], (D, 3 * D), D ** -0.5, 0.21875, ((1, 4),)),
        "heads_bias": bell_draw(arg_keys[6], (3 * D,), 0.3, 2.0, ((0, 4),), jnp.float32),
        "dense_weight": bell_draw(arg_keys[7], (D, D), (D // 16) ** -0.5, 0.875, ((0, 4),)),
        "dense_bias": bell_draw(arg_keys[8], (D,), 0.5, 3.0, (), jnp.float32),
        "second_gain": jnp.clip(1.0 + 0.18 * jax.random.normal(arg_keys[9], (D,), jnp.float32), 0.1, 1.9),
        "second_shift": bell_draw(arg_keys[10], (D,), 0.3, 2.0, (), jnp.float32),
        "expand_weight": bell_draw(arg_keys[11], (D, FF), D ** -0.5, 0.21875, ((1, 4),)),
        "expand_bias": bell_draw(arg_keys[12], (FF,), 0.5, 3.0, ((0, 4),), jnp.float32),
        "shrink_weight": bell_draw(arg_keys[13], (FF, D), FF ** -0.5, 0.109375, ((0, 4),)),
        "shrink_bias": bell_draw(arg_keys[14], (D,), 0.5, 3.0, (), jnp.float32),
        "cotangent": noise_with(arg_keys[15], (TOKENS, D), 1.0, 6.0, ((0, 32),), (0, 1, 32, 2.75)),
    }


epsilon = 1e-05
rotary_base = 10000.0
block_limit = 512

def contract(pattern, left_op, right_op):
    return jnp.einsum(pattern, left_op.astype(jnp.float32), right_op.astype(jnp.float32))

def layer_norm(wide_input):
    center = wide_input - lax.optimization_barrier(jnp.mean(wide_input, axis=-1, keepdims=True))
    norm_scale = lax.rsqrt(lax.optimization_barrier(jnp.mean(center * center, axis=-1, keepdims=True)) + epsilon)
    return (center * norm_scale, norm_scale)

def norm_backward(upstream, normed, norm_scale, gain_row):
    scaled = upstream * gain_row
    return norm_scale * (scaled - lax.optimization_barrier(jnp.mean(scaled, axis=-1, keepdims=True)) - normed * lax.optimization_barrier(jnp.mean(scaled * normed, axis=-1, keepdims=True)))

def gelu_value(hidden_pre):
    return hidden_pre * 0.5 * (1.0 + lax.erf(hidden_pre * (1.0 / math.sqrt(2.0))))

def gelu_slope(hidden_pre):
    return 0.5 * (1.0 + lax.erf(hidden_pre * (1.0 / math.sqrt(2.0)))) + hidden_pre * jnp.exp(-0.5 * hidden_pre * hidden_pre) * (1.0 / math.sqrt(2.0 * math.pi))

def rotary_tables(seq_positions):
    half_rot = ROT // 2
    frequency = rotary_base ** (jnp.arange(half_rot).astype(jnp.float32) * (-2.0 / ROT))
    angles = seq_positions.astype(jnp.float32)[:, None] * frequency[None, :]
    angles = jnp.concatenate([angles, angles], axis=1)
    return (jnp.cos(angles), jnp.sin(angles))

def half_turn(front_dims):
    half_rot = ROT // 2
    return jnp.concatenate([-front_dims[..., half_rot:], front_dims[..., :half_rot]], axis=-1)

def rotate_forward(vectors, cosine, sine_table):
    front_dims = vectors[..., :ROT]
    turned = front_dims * cosine[:, None, :] + half_turn(front_dims) * sine_table[:, None, :]
    return jnp.concatenate([turned, vectors[..., ROT:]], axis=-1)

def rotate_backward(upstream, cosine, sine_table):
    front_dims = upstream[..., :ROT]
    turned = front_dims * cosine[:, None, :] - half_turn(front_dims * sine_table[:, None, :])
    return jnp.concatenate([turned, upstream[..., ROT:]], axis=-1)

def mask_block(seq_segments, first_row, last_row):
    token_index = jnp.arange(last_row)
    causal_ok = token_index[first_row:last_row, None] >= token_index[None, :]
    same_doc = seq_segments[first_row:last_row, None] == seq_segments[None, :last_row]
    return causal_ok & same_doc

def block_scores(queries, key_rows, seq_segments, first_row, last_row):
    scores = contract('hqd,hkd->hqk', queries[:, first_row:last_row], key_rows[:, :last_row]) * (1.0 / math.sqrt(HD))
    return jnp.where(mask_block(seq_segments, first_row, last_row)[None], scores, -1e+30)

def attend_forward(queries, key_rows, value_rows, seq_segments):
    row_count = queries.shape[1]
    block_size = min(row_count, block_limit)
    context_parts = []
    logsum_parts = []
    for first_row in range(0, row_count, block_size):
        last_row = first_row + block_size
        scores = block_scores(queries, key_rows, seq_segments, first_row, last_row)
        row_max = lax.optimization_barrier(jnp.max(scores, axis=-1, keepdims=True))
        weights = jnp.exp(scores - row_max)
        row_total = lax.optimization_barrier(jnp.sum(weights, axis=-1, keepdims=True))
        weights_low = (weights / row_total).astype(jnp.bfloat16)
        context_parts.append(contract('hqk,hkd->hqd', weights_low, value_rows[:, :last_row]).astype(jnp.bfloat16))
        logsum_parts.append((row_max + jnp.log(row_total))[..., 0])
    return (jnp.concatenate(context_parts, axis=1), jnp.concatenate(logsum_parts, axis=1))

def attend_backward(queries, key_rows, value_rows, contexts, logsum, context_grad, seq_segments):
    row_count = queries.shape[1]
    block_size = min(row_count, block_limit)
    query_parts = []
    key_grad = jnp.zeros(key_rows.shape, jnp.float32)
    value_grad = jnp.zeros(value_rows.shape, jnp.float32)
    for first_row in range(0, row_count, block_size):
        last_row = first_row + block_size
        scores = block_scores(queries, key_rows, seq_segments, first_row, last_row)
        probs_back = jnp.exp(scores - logsum[:, first_row:last_row, None])
        probs_low = probs_back.astype(jnp.bfloat16)
        grad_block = context_grad[:, first_row:last_row]
        value_grad = value_grad.at[:, :last_row].add(contract('hqk,hqd->hkd', probs_low, grad_block))
        prob_grad = contract('hqd,hkd->hqk', grad_block, value_rows[:, :last_row])
        row_inner = lax.optimization_barrier(jnp.sum(grad_block.astype(jnp.float32) * contexts[:, first_row:last_row].astype(jnp.float32), axis=-1, keepdims=True))
        score_grad = (probs_back * (prob_grad - row_inner) * (1.0 / math.sqrt(HD))).astype(jnp.bfloat16)
        query_parts.append(contract('hqk,hkd->hqd', score_grad, key_rows[:, :last_row]))
        key_grad = key_grad.at[:, :last_row].add(contract('hqk,hqd->hkd', score_grad, queries[:, first_row:last_row]))
    return (jnp.concatenate(query_parts, axis=1), key_grad, value_grad)

def sequence_pass(tokens, seq_segments, seq_positions, upstream, params):
    first_gain, first_shift, heads_weight, heads_bias, dense_weight, dense_bias, second_gain, second_shift, expand_weight, expand_bias, shrink_weight, shrink_bias = params
    groups = N_TENSOR
    row_count = tokens.shape[0]
    head_count = heads_weight.shape[1] // (3 * HD)
    wide_input = tokens.astype(jnp.float32)
    normed, norm_scale = layer_norm(wide_input)
    first_input = (normed * first_gain + first_shift).astype(jnp.bfloat16)
    second_input = (normed * second_gain + second_shift).astype(jnp.bfloat16)
    mixed_rows = (jnp.dot(first_input, heads_weight, preferred_element_type=jnp.float32) + heads_bias).reshape(row_count, head_count, 3, HD)
    cosine, sine_table = rotary_tables(seq_positions)
    queries = rotate_forward(mixed_rows[:, :, 0], cosine, sine_table).astype(jnp.bfloat16).transpose(1, 0, 2)
    key_rows = rotate_forward(mixed_rows[:, :, 1], cosine, sine_table).astype(jnp.bfloat16).transpose(1, 0, 2)
    value_rows = mixed_rows[:, :, 2].astype(jnp.bfloat16).transpose(1, 0, 2)
    contexts, logsum = attend_forward(queries, key_rows, value_rows, seq_segments)
    context_rows = contexts.transpose(1, 0, 2).reshape(row_count, head_count * HD)
    hidden_pre = jnp.dot(second_input, expand_weight, preferred_element_type=jnp.float32) + expand_bias
    activated = gelu_value(hidden_pre).astype(jnp.bfloat16)
    attn_parts = contract('tgc,gcd->gtd', context_rows.reshape(row_count, groups, -1), dense_weight.reshape(groups, -1, D))
    feed_parts = contract('tgc,gcd->gtd', activated.reshape(row_count, groups, -1), shrink_weight.reshape(groups, -1, D))
    partial_value = attn_parts + feed_parts
    block_out = (wide_input + lax.optimization_barrier(jnp.sum(partial_value, axis=0)) + dense_bias + shrink_bias).astype(jnp.bfloat16)
    grad_rows = upstream.astype(jnp.float32)
    out_bias_grad = lax.optimization_barrier(jnp.sum(grad_rows, axis=0))
    shrink_grad = jnp.dot(activated.T, upstream, preferred_element_type=jnp.float32)
    pre_grad = jnp.dot(upstream, shrink_weight.T, preferred_element_type=jnp.float32) * gelu_slope(hidden_pre)
    expand_bias_grad = lax.optimization_barrier(jnp.sum(pre_grad, axis=0))
    pre_low = pre_grad.astype(jnp.bfloat16)
    expand_grad = jnp.dot(second_input.T, pre_low, preferred_element_type=jnp.float32)
    dense_grad = jnp.dot(context_rows.T, upstream, preferred_element_type=jnp.float32)
    context_grad = jnp.dot(upstream, dense_weight.T, preferred_element_type=jnp.float32).astype(jnp.bfloat16)
    context_grad = context_grad.reshape(row_count, head_count, HD).transpose(1, 0, 2)
    query_grad, key_grad, value_grad = attend_backward(queries, key_rows, value_rows, contexts, logsum, context_grad, seq_segments)
    query_grad = rotate_backward(query_grad.transpose(1, 0, 2), cosine, sine_table)
    key_grad = rotate_backward(key_grad.transpose(1, 0, 2), cosine, sine_table)
    mixed_grad = jnp.stack([query_grad, key_grad, value_grad.transpose(1, 0, 2)], axis=2).reshape(row_count, head_count * 3 * HD)
    heads_bias_grad = lax.optimization_barrier(jnp.sum(mixed_grad, axis=0))
    mixed_low = mixed_grad.astype(jnp.bfloat16)
    heads_grad = jnp.dot(first_input.T, mixed_low, preferred_element_type=jnp.float32)
    first_parts = contract('tgc,dgc->gtd', mixed_low.reshape(row_count, groups, -1), heads_weight.reshape(D, groups, -1))
    second_parts = contract('tgc,dgc->gtd', pre_low.reshape(row_count, groups, -1), expand_weight.reshape(D, groups, -1))
    input_part = norm_backward(first_parts, normed, norm_scale, first_gain) + norm_backward(second_parts, normed, norm_scale, second_gain)
    block_back = (grad_rows + lax.optimization_barrier(jnp.sum(input_part, axis=0))).astype(jnp.bfloat16)
    first_up = lax.optimization_barrier(jnp.sum(first_parts, axis=0))
    second_up = lax.optimization_barrier(jnp.sum(second_parts, axis=0))
    gradients = (lax.optimization_barrier(jnp.sum(first_up * normed, axis=0)), lax.optimization_barrier(jnp.sum(first_up, axis=0)), heads_grad, heads_bias_grad, dense_grad, out_bias_grad, lax.optimization_barrier(jnp.sum(second_up * normed, axis=0)), lax.optimization_barrier(jnp.sum(second_up, axis=0)), expand_grad, expand_bias_grad, shrink_grad)
    return (block_out, block_back, gradients)

def reference(hidden_in, segments, positions, first_gain, first_shift, heads_weight, heads_bias, dense_weight, dense_bias, second_gain, second_shift, expand_weight, expand_bias, shrink_weight, shrink_bias, cotangent):
    params = (first_gain, first_shift, heads_weight, heads_bias, dense_weight, dense_bias, second_gain, second_shift, expand_weight, expand_bias, shrink_weight, shrink_bias)
    seq_total = TOKENS // LEN

    def one_sequence(running, inputs):
        tokens, seq_segments, seq_positions, upstream = inputs
        block_out, block_back, gradients = sequence_pass(tokens, seq_segments, seq_positions, upstream, params)
        return (jax.tree.map(jnp.add, running, gradients), (block_out, block_back))
    initial = (jnp.zeros((D,), jnp.float32), jnp.zeros((D,), jnp.float32), jnp.zeros((D, 3 * D), jnp.float32), jnp.zeros((3 * D,), jnp.float32), jnp.zeros((D, D), jnp.float32), jnp.zeros((D,), jnp.float32), jnp.zeros((D,), jnp.float32), jnp.zeros((D,), jnp.float32), jnp.zeros((D, FF), jnp.float32), jnp.zeros((FF,), jnp.float32), jnp.zeros((FF, D), jnp.float32))
    inputs = (hidden_in.reshape(seq_total, LEN, D), segments.reshape(seq_total, LEN), positions.reshape(seq_total, LEN), cotangent.reshape(seq_total, LEN, D))
    totals, outputs = lax.scan(one_sequence, initial, inputs)
    hidden_out = outputs[0].reshape(TOKENS, D)
    hidden_gradient = outputs[1].reshape(TOKENS, D)
    return (hidden_out, hidden_gradient, totals[0], totals[1], totals[2], totals[3], totals[4], totals[5], totals[6], totals[7], totals[8], totals[9], totals[10], totals[5])
```

```python
import math

import jax
import jax.numpy as jnp
from jax import lax
from jax.sharding import PartitionSpec as P

HD = 64
ROT = 16


epsilon = 1e-05
rotary_base = 10000.0
block_limit = 512


def contract(pattern, left_op, right_op):
    return jnp.einsum(pattern, left_op, right_op, preferred_element_type=jnp.float32)


def layer_norm(wide_input):
    center = wide_input - jnp.mean(wide_input, axis=-1, keepdims=True)
    norm_scale = lax.rsqrt(jnp.mean(center * center, axis=-1, keepdims=True) + epsilon)
    return (center * norm_scale, norm_scale)


def norm_backward(upstream, normed, norm_scale, gain_row):
    scaled = upstream * gain_row
    return norm_scale * (
        scaled
        - jnp.mean(scaled, axis=-1, keepdims=True)
        - normed * jnp.mean(scaled * normed, axis=-1, keepdims=True)
    )


def gelu_value(hidden_pre):
    return hidden_pre * 0.5 * (1.0 + lax.erf(hidden_pre * (1.0 / math.sqrt(2.0))))


def gelu_slope(hidden_pre):
    return 0.5 * (1.0 + lax.erf(hidden_pre * (1.0 / math.sqrt(2.0)))) + hidden_pre * jnp.exp(
        -0.5 * hidden_pre * hidden_pre
    ) * (1.0 / math.sqrt(2.0 * math.pi))


def rotary_tables(seq_positions):
    half_rot = ROT // 2
    frequency = rotary_base ** (jnp.arange(half_rot).astype(jnp.float32) * (-2.0 / ROT))
    angles = seq_positions.astype(jnp.float32)[:, None] * frequency[None, :]
    angles = jnp.concatenate([angles, angles], axis=1)
    return (jnp.cos(angles), jnp.sin(angles))


def half_turn(front_dims):
    half_rot = ROT // 2
    return jnp.concatenate([-front_dims[..., half_rot:], front_dims[..., :half_rot]], axis=-1)


def rotate_forward(vectors, cosine, sine_table):
    front_dims = vectors[..., :ROT]
    turned = front_dims * cosine[:, None, :] + half_turn(front_dims) * sine_table[:, None, :]
    return jnp.concatenate([turned, vectors[..., ROT:]], axis=-1)


def rotate_backward(upstream, cosine, sine_table):
    front_dims = upstream[..., :ROT]
    turned = front_dims * cosine[:, None, :] - half_turn(front_dims * sine_table[:, None, :])
    return jnp.concatenate([turned, upstream[..., ROT:]], axis=-1)


def mask_block(seq_segments, first_row, last_row):
    token_index = jnp.arange(last_row)
    causal_ok = token_index[first_row:last_row, None] >= token_index[None, :]
    same_doc = seq_segments[first_row:last_row, None] == seq_segments[None, :last_row]
    return causal_ok & same_doc


def block_scores(queries, key_rows, seq_segments, first_row, last_row):
    scores = contract("hqd,hkd->hqk", queries[:, first_row:last_row], key_rows[:, :last_row]) * (
        1.0 / math.sqrt(HD)
    )
    return jnp.where(mask_block(seq_segments, first_row, last_row)[None], scores, -1e30)


def attend_forward(queries, key_rows, value_rows, seq_segments):
    row_count = queries.shape[1]
    block_size = min(row_count, block_limit)
    context_parts = []
    logsum_parts = []
    for first_row in range(0, row_count, block_size):
        last_row = first_row + block_size
        scores = block_scores(queries, key_rows, seq_segments, first_row, last_row)
        row_max = jnp.max(scores, axis=-1, keepdims=True)
        weights = jnp.exp(scores - row_max)
        row_total = jnp.sum(weights, axis=-1, keepdims=True)
        weights_low = (weights / row_total).astype(jnp.bfloat16)
        context_parts.append(
            contract("hqk,hkd->hqd", weights_low, value_rows[:, :last_row]).astype(jnp.bfloat16)
        )
        logsum_parts.append((row_max + jnp.log(row_total))[..., 0])
    return (jnp.concatenate(context_parts, axis=1), jnp.concatenate(logsum_parts, axis=1))


def attend_backward(queries, key_rows, value_rows, contexts, logsum, context_grad, seq_segments):
    row_count = queries.shape[1]
    block_size = min(row_count, block_limit)
    query_parts = []
    key_grad = jnp.zeros(key_rows.shape, jnp.float32)
    value_grad = jnp.zeros(value_rows.shape, jnp.float32)
    for first_row in range(0, row_count, block_size):
        last_row = first_row + block_size
        scores = block_scores(queries, key_rows, seq_segments, first_row, last_row)
        probs_back = jnp.exp(scores - logsum[:, first_row:last_row, None])
        probs_low = probs_back.astype(jnp.bfloat16)
        grad_block = context_grad[:, first_row:last_row]
        value_grad = value_grad.at[:, :last_row].add(
            contract("hqk,hqd->hkd", probs_low, grad_block)
        )
        prob_grad = contract("hqd,hkd->hqk", grad_block, value_rows[:, :last_row])
        row_inner = jnp.sum(
            grad_block.astype(jnp.float32) * contexts[:, first_row:last_row].astype(jnp.float32),
            axis=-1,
            keepdims=True,
        )
        score_grad = (probs_back * (prob_grad - row_inner) * (1.0 / math.sqrt(HD))).astype(
            jnp.bfloat16
        )
        query_parts.append(contract("hqk,hkd->hqd", score_grad, key_rows[:, :last_row]))
        key_grad = key_grad.at[:, :last_row].add(
            contract("hqk,hqd->hkd", score_grad, queries[:, first_row:last_row])
        )
    return (jnp.concatenate(query_parts, axis=1), key_grad, value_grad)


N_DP = 32
N_TENSOR = 4


def pair_list(partner):
    pairs = []
    for row in range(N_DP):
        for col in range(N_TENSOR):
            to_row, to_col = partner(row, col)
            pairs.append((row * N_TENSOR + col, to_row * N_TENSOR + to_col))
    return pairs


def swap(values, masks, axis):
    if axis == "tensor":
        pairs = pair_list(lambda row, col: (row, col ^ masks[row & 1]))
    else:
        pairs = pair_list(lambda row, col: (row ^ masks[row & 1], col))
    return lax.ppermute(values, ("dp", "tensor"), pairs)


def half_of(values, which, axis=0):
    size = values.shape[axis] // 2
    return lax.dynamic_slice_in_dim(values, which * size, size, axis)


def joined(which, own, other, axis=0):
    return jnp.where(
        which == 0,
        jnp.concatenate([own, other], axis=axis),
        jnp.concatenate([other, own], axis=axis),
    )


def tensor_phases():
    core = lax.axis_index("dp") & 1
    place = lax.axis_index("tensor")
    low, high = place & 1, place >> 1
    return [
        ((1, 3), jnp.where(core == 0, low ^ high, high), 0),
        ((3, 1), jnp.where(core == 0, high, low), 0),
    ]


def dp_phases(orders):
    index = lax.axis_index("dp")
    core = index & 1
    bit = [(index >> place) & 1 for place in range(5)]

    def keeps(order):
        seen, keep = set(), []
        for mask in order:
            if mask == 2:
                keep.append(bit[1] if 6 in seen else bit[1] ^ bit[2])
            elif mask == 6:
                keep.append(bit[2])
            elif mask == 8:
                keep.append(bit[3] if 24 in seen else bit[3] ^ bit[4])
            else:
                keep.append(bit[4])
            seen.add(mask)
        return keep

    first, second = keeps(orders[0]), keeps(orders[1])
    phases = [((1, 1), core, 1)]
    for step in range(4):
        masks = (orders[0][step], orders[1][step])
        phases.append((masks, jnp.where(core == 0, first[step], second[step]), 0))
    return phases


def after(values, *earlier):
    return lax.optimization_barrier((values, earlier))[0]


class Exchange:
    def __init__(self, phases, halve, axis_name):
        self.axis = axis_name
        steps = [("halve", p) for p in phases[:halve]] + [("sum", p) for p in phases[halve:]]
        self.steps = steps + [("join", p) for p in phases[:halve][::-1]]
        self.values = None
        self.flying = None

    def put(self, values):
        self.values = values
        return self

    def put_halves(self, own, other):
        self.values = own
        self.flying = swap(other, self.steps[0][1][0], self.axis)
        return self

    def send(self):
        kind, (masks, keep, split) = self.steps[0]
        outgoing = half_of(self.values, 1 - keep, split) if kind == "halve" else self.values
        self.flying = swap(outgoing, masks, self.axis)
        if kind == "halve":
            self.values = half_of(self.values, keep, split)
        return self

    def land(self, *earlier):
        kind, (masks, keep, split) = self.steps.pop(0)
        arrived = after(self.flying, *earlier) if earlier else self.flying
        if kind == "join":
            self.values = joined(keep, self.values, arrived, split)
        else:
            self.values = self.values + arrived
        if self.steps:
            self.send()
        return self.values

    def finish(self):
        while self.steps:
            self.land()
        return self.values


def on_device(
    hidden_in,
    segments,
    positions,
    first_gain,
    first_shift,
    heads_weight,
    heads_bias,
    dense_weight,
    dense_bias,
    second_gain,
    second_shift,
    expand_weight,
    expand_bias,
    shrink_weight,
    shrink_bias,
    cotangent,
):
    row_count, width = hidden_in.shape
    columns = heads_weight.shape[1]
    head_count = columns // (3 * HD)
    units = expand_weight.shape[1]
    context_width = head_count * HD
    half = row_count // 2
    core = lax.axis_index("dp") & 1
    y_phases = tensor_phases()
    early_phases = dp_phases(((8, 2, 24, 6), (2, 8, 6, 24)))
    late_phases = dp_phases(((24, 6, 8, 2), (6, 24, 2, 8)))
    cosine, sine_table = rotary_tables(positions)

    wide_input = hidden_in.astype(jnp.float32)
    normed, norm_scale = layer_norm(wide_input)
    first_input = (normed * first_gain + first_shift).astype(jnp.bfloat16)
    second_input = (normed * second_gain + second_shift).astype(jnp.bfloat16)
    mixed_rows = (
        jnp.dot(first_input, heads_weight, preferred_element_type=jnp.float32) + heads_bias
    ).reshape(row_count, head_count, 3, HD)
    queries = (
        rotate_forward(mixed_rows[:, :, 0], cosine, sine_table)
        .astype(jnp.bfloat16)
        .transpose(1, 0, 2)
    )
    key_rows = (
        rotate_forward(mixed_rows[:, :, 1], cosine, sine_table)
        .astype(jnp.bfloat16)
        .transpose(1, 0, 2)
    )
    value_rows = mixed_rows[:, :, 2].astype(jnp.bfloat16).transpose(1, 0, 2)
    contexts, logsum = attend_forward(queries, key_rows, value_rows, segments)
    context_rows = contexts.transpose(1, 0, 2).reshape(row_count, context_width)
    hidden_pre = (
        jnp.dot(second_input, expand_weight, preferred_element_type=jnp.float32) + expand_bias
    )
    activated = gelu_value(hidden_pre).astype(jnp.bfloat16)

    keep = y_phases[0][1]

    def branch_rows(which):
        part = jnp.dot(
            half_of(context_rows, which), dense_weight, preferred_element_type=jnp.float32
        )
        return part + jnp.dot(
            half_of(activated, which), shrink_weight, preferred_element_type=jnp.float32
        )

    part_other = branch_rows(1 - keep)
    part_own = branch_rows(keep)
    out = Exchange(y_phases, 1, "tensor").put_halves(part_own, part_other)

    upstream = after(cotangent, part_own)
    pre_grad = jnp.dot(upstream, shrink_weight.T, preferred_element_type=jnp.float32) * gelu_slope(
        hidden_pre
    )
    pre_low = pre_grad.astype(jnp.bfloat16)
    ones = (jnp.arange(32) == 0).astype(jnp.bfloat16)[None, :] * jnp.ones(
        (row_count, 1), jnp.bfloat16
    )
    output_side = jnp.concatenate([activated, context_rows, ones], axis=1)
    input_side = jnp.concatenate([second_input, ones], axis=1)

    def early_columns(which):
        parts = [
            jnp.dot(left.T, half_of(right, which, 1), preferred_element_type=jnp.float32)
            for left, right in ((output_side, upstream), (input_side, pre_low))
        ]
        return jnp.concatenate(parts, axis=0)

    early_other = early_columns(1 - core)
    early_own = early_columns(core)
    early = Exchange(early_phases, 3, "dp").put_halves(early_own, early_other)
    landed = [out.land(early_own)]

    context_grad = jnp.dot(
        after(cotangent, landed), dense_weight.T, preferred_element_type=jnp.float32
    ).astype(jnp.bfloat16)
    context_grad = context_grad.reshape(row_count, head_count, HD).transpose(1, 0, 2)
    landed = [early.land(context_grad)]
    query_grad, key_grad, value_grad = attend_backward(
        queries, key_rows, value_rows, contexts, logsum, after(context_grad, landed), segments
    )
    landed = [out.land(query_grad), early.land(query_grad)]
    query_grad = after(query_grad, landed)
    query_grad = rotate_backward(query_grad.transpose(1, 0, 2), cosine, sine_table)
    key_grad = rotate_backward(key_grad.transpose(1, 0, 2), cosine, sine_table)
    mixed_grad = jnp.stack([query_grad, key_grad, value_grad.transpose(1, 0, 2)], axis=2).reshape(
        row_count, columns
    )
    mixed_low = mixed_grad.astype(jnp.bfloat16)
    first_up = jnp.dot(mixed_low, heads_weight.T, preferred_element_type=jnp.float32)
    second_up = jnp.dot(pre_low, expand_weight.T, preferred_element_type=jnp.float32)
    input_part = norm_backward(first_up, normed, norm_scale, first_gain) + norm_backward(
        second_up, normed, norm_scale, second_gain
    )
    back = Exchange(y_phases, 1, "tensor").put(input_part).send()

    sums = jnp.stack(
        [
            jnp.sum(first_up * normed, axis=0),
            jnp.sum(first_up, axis=0),
            jnp.sum(second_up * normed, axis=0),
            jnp.sum(second_up, axis=0),
            jnp.pad(jnp.sum(mixed_grad, axis=0), (0, width - columns)),
        ]
    )
    sums = jnp.pad(sums, ((0, 59), (0, 0)))

    def late_columns(which):
        part = jnp.dot(
            mixed_low.T, half_of(first_input, which, 1), preferred_element_type=jnp.float32
        )
        return jnp.concatenate([part, half_of(sums, which, 1)], axis=0)

    late_other = late_columns(1 - core)
    late_own = late_columns(core)
    late = Exchange(late_phases, 3, "dp").put_halves(late_own, late_other)
    landed = early.land(late_own)
    landed = late.land(landed)
    landed = out.land(landed)
    landed = late.land(landed)
    landed = early.land(landed)
    landed = back.land(landed)
    landed = late.land(landed)
    landed = early.land(landed)
    landed = late.land(landed)
    landed = late.land(landed)
    landed = early.land(landed)
    landed = back.land(landed)
    landed = late.finish()
    early.finish()
    back.finish()

    hidden_out = (wide_input + out.values + dense_bias + shrink_bias).astype(jnp.bfloat16)
    hidden_gradient = (cotangent.astype(jnp.float32) + back.values).astype(jnp.bfloat16)
    early, late = early.values, late.values
    norm_terms = late[columns : columns + 8]
    for mask in (1, 3):
        norm_terms = norm_terms + swap(norm_terms, (mask, mask), "tensor")
    dense_row = units + context_width
    out_bias_grad = early[dense_row]
    expand_row = dense_row + 32
    return (
        hidden_out,
        hidden_gradient,
        norm_terms[0],
        norm_terms[1],
        late[:columns].T,
        late[columns + 4, :columns],
        early[units:dense_row],
        out_bias_grad,
        norm_terms[2],
        norm_terms[3],
        early[expand_row : expand_row + width],
        early[expand_row + width],
        early[:units],
        out_bias_grad,
    )


def solution(mesh):
    placed = (
        P("dp", None),
        P("dp"),
        P("dp"),
        P(),
        P(),
        P(None, "tensor"),
        P("tensor"),
        P("tensor", None),
        P(),
        P(),
        P(),
        P(None, "tensor"),
        P("tensor"),
        P("tensor", None),
        P(),
        P("dp", None),
    )
    return jax.shard_map(
        on_device,
        mesh=mesh,
        in_specs=placed,
        out_specs=(
            P("dp", None),
            P("dp", None),
            P(),
            P(),
            P(None, "tensor"),
            P("tensor"),
            P("tensor", None),
            P(),
            P(),
            P(),
            P(None, "tensor"),
            P("tensor"),
            P("tensor", None),
            P(),
        ),
        check_vma=False,
    )
```

```python
import math

import jax
import jax.numpy as jnp
from jax import lax
from jax.sharding import PartitionSpec as P

HD = 64
ROT = 16


epsilon = 1e-05
rotary_base = 10000.0
block_limit = 512


def contract(pattern, left_op, right_op):
    return jnp.einsum(pattern, left_op, right_op, preferred_element_type=jnp.float32)


def layer_norm(wide_input):
    center = wide_input - jnp.mean(wide_input, axis=-1, keepdims=True)
    norm_scale = lax.rsqrt(jnp.mean(center * center, axis=-1, keepdims=True) + epsilon)
    return (center * norm_scale, norm_scale)


def norm_backward(upstream, normed, norm_scale, gain_row):
    scaled = upstream * gain_row
    return norm_scale * (
        scaled
        - jnp.mean(scaled, axis=-1, keepdims=True)
        - normed * jnp.mean(scaled * normed, axis=-1, keepdims=True)
    )


def gelu_value(hidden_pre):
    return hidden_pre * 0.5 * (1.0 + lax.erf(hidden_pre * (1.0 / math.sqrt(2.0))))


def gelu_slope(hidden_pre):
    return 0.5 * (1.0 + lax.erf(hidden_pre * (1.0 / math.sqrt(2.0)))) + hidden_pre * jnp.exp(
        -0.5 * hidden_pre * hidden_pre
    ) * (1.0 / math.sqrt(2.0 * math.pi))


def rotary_tables(seq_positions):
    half_rot = ROT // 2
    frequency = rotary_base ** (jnp.arange(half_rot).astype(jnp.float32) * (-2.0 / ROT))
    angles = seq_positions.astype(jnp.float32)[:, None] * frequency[None, :]
    angles = jnp.concatenate([angles, angles], axis=1)
    return (jnp.cos(angles), jnp.sin(angles))


def half_turn(front_dims):
    half_rot = ROT // 2
    return jnp.concatenate([-front_dims[..., half_rot:], front_dims[..., :half_rot]], axis=-1)


def rotate_forward(vectors, cosine, sine_table):
    front_dims = vectors[..., :ROT]
    turned = front_dims * cosine[:, None, :] + half_turn(front_dims) * sine_table[:, None, :]
    return jnp.concatenate([turned, vectors[..., ROT:]], axis=-1)


def rotate_backward(upstream, cosine, sine_table):
    front_dims = upstream[..., :ROT]
    turned = front_dims * cosine[:, None, :] - half_turn(front_dims * sine_table[:, None, :])
    return jnp.concatenate([turned, upstream[..., ROT:]], axis=-1)


def mask_block(seq_segments, first_row, last_row):
    token_index = jnp.arange(last_row)
    causal_ok = token_index[first_row:last_row, None] >= token_index[None, :]
    same_doc = seq_segments[first_row:last_row, None] == seq_segments[None, :last_row]
    return causal_ok & same_doc


def block_scores(queries, key_rows, seq_segments, first_row, last_row):
    scores = contract("hqd,hkd->hqk", queries[:, first_row:last_row], key_rows[:, :last_row]) * (
        1.0 / math.sqrt(HD)
    )
    return jnp.where(mask_block(seq_segments, first_row, last_row)[None], scores, -1e30)


def attend_forward(queries, key_rows, value_rows, seq_segments):
    row_count = queries.shape[1]
    block_size = min(row_count, block_limit)
    context_parts = []
    logsum_parts = []
    for first_row in range(0, row_count, block_size):
        last_row = first_row + block_size
        scores = block_scores(queries, key_rows, seq_segments, first_row, last_row)
        row_max = jnp.max(scores, axis=-1, keepdims=True)
        weights = jnp.exp(scores - row_max)
        row_total = jnp.sum(weights, axis=-1, keepdims=True)
        weights_low = (weights / row_total).astype(jnp.bfloat16)
        context_parts.append(
            contract("hqk,hkd->hqd", weights_low, value_rows[:, :last_row]).astype(jnp.bfloat16)
        )
        logsum_parts.append((row_max + jnp.log(row_total))[..., 0])
    return (jnp.concatenate(context_parts, axis=1), jnp.concatenate(logsum_parts, axis=1))


def attend_backward(queries, key_rows, value_rows, contexts, logsum, context_grad, seq_segments):
    row_count = queries.shape[1]
    block_size = min(row_count, block_limit)
    query_parts = []
    key_grad = jnp.zeros(key_rows.shape, jnp.float32)
    value_grad = jnp.zeros(value_rows.shape, jnp.float32)
    for first_row in range(0, row_count, block_size):
        last_row = first_row + block_size
        scores = block_scores(queries, key_rows, seq_segments, first_row, last_row)
        probs_back = jnp.exp(scores - logsum[:, first_row:last_row, None])
        probs_low = probs_back.astype(jnp.bfloat16)
        grad_block = context_grad[:, first_row:last_row]
        value_grad = value_grad.at[:, :last_row].add(
            contract("hqk,hqd->hkd", probs_low, grad_block)
        )
        prob_grad = contract("hqd,hkd->hqk", grad_block, value_rows[:, :last_row])
        row_inner = jnp.sum(
            grad_block.astype(jnp.float32) * contexts[:, first_row:last_row].astype(jnp.float32),
            axis=-1,
            keepdims=True,
        )
        score_grad = (probs_back * (prob_grad - row_inner) * (1.0 / math.sqrt(HD))).astype(
            jnp.bfloat16
        )
        query_parts.append(contract("hqk,hkd->hqd", score_grad, key_rows[:, :last_row]))
        key_grad = key_grad.at[:, :last_row].add(
            contract("hqk,hqd->hkd", score_grad, queries[:, first_row:last_row])
        )
    return (jnp.concatenate(query_parts, axis=1), key_grad, value_grad)


N_DP = 32
N_TENSOR = 4


def pair_list(partner):
    pairs = []
    for row in range(N_DP):
        for col in range(N_TENSOR):
            to_row, to_col = partner(row, col)
            pairs.append((row * N_TENSOR + col, to_row * N_TENSOR + to_col))
    return pairs


def swap(values, masks, axis):
    if axis == "tensor":
        pairs = pair_list(lambda row, col: (row, col ^ masks[row & 1]))
    else:
        pairs = pair_list(lambda row, col: (row ^ masks[row & 1], col))
    return lax.ppermute(values, ("dp", "tensor"), pairs)


def half_of(values, which, axis=0):
    size = values.shape[axis] // 2
    return lax.dynamic_slice_in_dim(values, which * size, size, axis)


def joined(which, own, other, axis=0):
    return jnp.where(
        which == 0,
        jnp.concatenate([own, other], axis=axis),
        jnp.concatenate([other, own], axis=axis),
    )


def tensor_phases():
    core = lax.axis_index("dp") & 1
    place = lax.axis_index("tensor")
    low, high = place & 1, place >> 1
    return [
        ((1, 3), jnp.where(core == 0, low ^ high, high), 0),
        ((3, 1), jnp.where(core == 0, high, low), 0),
    ]


def dp_phases(orders):
    index = lax.axis_index("dp")
    core = index & 1
    bit = [(index >> place) & 1 for place in range(5)]

    def keeps(order):
        seen, keep = set(), []
        for mask in order:
            if mask == 2:
                keep.append(bit[1] if 6 in seen else bit[1] ^ bit[2])
            elif mask == 6:
                keep.append(bit[2])
            elif mask == 8:
                keep.append(bit[3] if 24 in seen else bit[3] ^ bit[4])
            else:
                keep.append(bit[4])
            seen.add(mask)
        return keep

    first, second = keeps(orders[0]), keeps(orders[1])
    phases = [((1, 1), core, 1)]
    for step in range(4):
        masks = (orders[0][step], orders[1][step])
        phases.append((masks, jnp.where(core == 0, first[step], second[step]), 0))
    return phases


def after(values, *earlier):
    return lax.optimization_barrier((values, earlier))[0]


class Exchange:
    def __init__(self, phases, halve, axis_name):
        self.axis = axis_name
        steps = [("halve", p) for p in phases[:halve]] + [("sum", p) for p in phases[halve:]]
        self.steps = steps + [("join", p) for p in phases[:halve][::-1]]
        self.values = None
        self.flying = None

    def put(self, values):
        self.values = values
        return self

    def put_halves(self, own, other):
        self.values = own
        self.flying = swap(other, self.steps[0][1][0], self.axis)
        return self

    def send(self):
        kind, (masks, keep, split) = self.steps[0]
        outgoing = half_of(self.values, 1 - keep, split) if kind == "halve" else self.values
        self.flying = swap(outgoing, masks, self.axis)
        if kind == "halve":
            self.values = half_of(self.values, keep, split)
        return self

    def land(self, *earlier):
        kind, (masks, keep, split) = self.steps.pop(0)
        arrived = after(self.flying, *earlier) if earlier else self.flying
        if kind == "join":
            self.values = joined(keep, self.values, arrived, split)
        else:
            self.values = self.values + arrived
        if self.steps:
            self.send()
        return self.values

    def finish(self):
        while self.steps:
            self.land()
        return self.values


def on_device(
    hidden_in,
    segments,
    positions,
    first_gain,
    first_shift,
    heads_weight,
    heads_bias,
    dense_weight,
    dense_bias,
    second_gain,
    second_shift,
    expand_weight,
    expand_bias,
    shrink_weight,
    shrink_bias,
    cotangent,
):
    row_count, width = hidden_in.shape
    columns = heads_weight.shape[1]
    head_count = columns // (3 * HD)
    units = expand_weight.shape[1]
    context_width = head_count * HD
    half = row_count // 2
    core = lax.axis_index("dp") & 1
    y_phases = tensor_phases()
    early_phases = dp_phases(((8, 2, 24, 6), (2, 8, 6, 24)))
    late_phases = dp_phases(((24, 6, 8, 2), (6, 24, 2, 8)))
    cosine, sine_table = rotary_tables(positions)

    wide_input = hidden_in.astype(jnp.float32)
    normed, norm_scale = layer_norm(wide_input)
    first_input = (normed * first_gain + first_shift).astype(jnp.bfloat16)
    second_input = (normed * second_gain + second_shift).astype(jnp.bfloat16)
    mixed_rows = (
        jnp.dot(first_input, heads_weight, preferred_element_type=jnp.float32) + heads_bias
    ).reshape(row_count, head_count, 3, HD)
    queries = (
        rotate_forward(mixed_rows[:, :, 0], cosine, sine_table)
        .astype(jnp.bfloat16)
        .transpose(1, 0, 2)
    )
    key_rows = (
        rotate_forward(mixed_rows[:, :, 1], cosine, sine_table)
        .astype(jnp.bfloat16)
        .transpose(1, 0, 2)
    )
    value_rows = mixed_rows[:, :, 2].astype(jnp.bfloat16).transpose(1, 0, 2)
    contexts, logsum = attend_forward(queries, key_rows, value_rows, segments)
    context_rows = contexts.transpose(1, 0, 2).reshape(row_count, context_width)
    hidden_pre = (
        jnp.dot(second_input, expand_weight, preferred_element_type=jnp.float32) + expand_bias
    )
    activated = gelu_value(hidden_pre).astype(jnp.bfloat16)

    keep = y_phases[0][1]

    def branch_rows(which):
        part = jnp.dot(
            half_of(context_rows, which), dense_weight, preferred_element_type=jnp.float32
        )
        return part + jnp.dot(
            half_of(activated, which), shrink_weight, preferred_element_type=jnp.float32
        )

    part_other = branch_rows(1 - keep)
    part_own = branch_rows(keep)
    out = Exchange(y_phases, 1, "tensor").put_halves(part_own, part_other)

    upstream = after(cotangent, part_own)
    pre_grad = jnp.dot(upstream, shrink_weight.T, preferred_element_type=jnp.float32) * gelu_slope(
        hidden_pre
    )
    pre_low = pre_grad.astype(jnp.bfloat16)
    ones = (jnp.arange(32) == 0).astype(jnp.bfloat16)[None, :] * jnp.ones(
        (row_count, 1), jnp.bfloat16
    )
    output_side = jnp.concatenate([activated, context_rows, ones], axis=1)
    input_side = jnp.concatenate([second_input, ones], axis=1)

    def early_columns(which):
        parts = [
            jnp.dot(left.T, half_of(right, which, 1), preferred_element_type=jnp.float32)
            for left, right in ((output_side, upstream), (input_side, pre_low))
        ]
        return jnp.concatenate(parts, axis=0)

    early_other = early_columns(1 - core)
    early_own = early_columns(core)
    early = Exchange(early_phases, 3, "dp").put_halves(early_own, early_other)

    context_grad = jnp.dot(
        after(cotangent, early_own), dense_weight.T, preferred_element_type=jnp.float32
    ).astype(jnp.bfloat16)
    context_grad = context_grad.reshape(row_count, head_count, HD).transpose(1, 0, 2)
    landed = [early.land(context_grad)]
    query_grad, key_grad, value_grad = attend_backward(
        queries, key_rows, value_rows, contexts, logsum, after(context_grad, landed), segments
    )
    landed = [out.land(query_grad), early.land(query_grad)]
    query_grad = after(query_grad, landed)
    query_grad = rotate_backward(query_grad.transpose(1, 0, 2), cosine, sine_table)
    key_grad = rotate_backward(key_grad.transpose(1, 0, 2), cosine, sine_table)
    mixed_grad = jnp.stack([query_grad, key_grad, value_grad.transpose(1, 0, 2)], axis=2).reshape(
        row_count, columns
    )
    mixed_low = mixed_grad.astype(jnp.bfloat16)
    landed = early.land(mixed_low)
    first_up = jnp.dot(
        after(mixed_low, landed), heads_weight.T, preferred_element_type=jnp.float32
    )
    landed = out.land(first_up)
    second_up = jnp.dot(
        after(pre_low, landed), expand_weight.T, preferred_element_type=jnp.float32
    )
    input_part = norm_backward(first_up, normed, norm_scale, first_gain) + norm_backward(
        second_up, normed, norm_scale, second_gain
    )
    back = Exchange(y_phases, 1, "tensor").put(input_part).send()

    sums = jnp.stack(
        [
            jnp.sum(first_up * normed, axis=0),
            jnp.sum(first_up, axis=0),
            jnp.sum(second_up * normed, axis=0),
            jnp.sum(second_up, axis=0),
            jnp.pad(jnp.sum(mixed_grad, axis=0), (0, width - columns)),
        ]
    )
    sums = jnp.pad(sums, ((0, 59), (0, 0)))

    def late_columns(which):
        part = jnp.dot(
            mixed_low.T, half_of(first_input, which, 1), preferred_element_type=jnp.float32
        )
        return jnp.concatenate([part, half_of(sums, which, 1)], axis=0)

    late_other = late_columns(1 - core)
    late_own = late_columns(core)
    late = Exchange(late_phases, 3, "dp").put_halves(late_own, late_other)
    landed = early.land(late_own)
    landed = late.land(landed)
    landed = out.land(landed)
    landed = late.land(landed)
    landed = early.land(landed)
    landed = back.land(landed)
    landed = late.land(landed)
    landed = late.land(landed)
    landed = early.land(landed)
    landed = late.land(landed)
    landed = late.land(landed)
    landed = back.land(landed)
    landed = late.land(landed)
    landed = early.land(landed)
    late.finish()
    early.finish()
    back.finish()

    hidden_out = (wide_input + out.values + dense_bias + shrink_bias).astype(jnp.bfloat16)
    hidden_gradient = (cotangent.astype(jnp.float32) + back.values).astype(jnp.bfloat16)
    early, late = early.values, late.values
    norm_terms = late[columns : columns + 8]
    for mask in (1, 3):
        norm_terms = norm_terms + swap(norm_terms, (mask, mask), "tensor")
    dense_row = units + context_width
    out_bias_grad = early[dense_row]
    expand_row = dense_row + 32
    return (
        hidden_out,
        hidden_gradient,
        norm_terms[0],
        norm_terms[1],
        late[:columns].T,
        late[columns + 4, :columns],
        early[units:dense_row],
        out_bias_grad,
        norm_terms[2],
        norm_terms[3],
        early[expand_row : expand_row + width],
        early[expand_row + width],
        early[:units],
        out_bias_grad,
    )


def solution(mesh):
    placed = (
        P("dp", None),
        P("dp"),
        P("dp"),
        P(),
        P(),
        P(None, "tensor"),
        P("tensor"),
        P("tensor", None),
        P(),
        P(),
        P(),
        P(None, "tensor"),
        P("tensor"),
        P("tensor", None),
        P(),
        P("dp", None),
    )
    return jax.shard_map(
        on_device,
        mesh=mesh,
        in_specs=placed,
        out_specs=(
            P("dp", None),
            P("dp", None),
            P(),
            P(),
            P(None, "tensor"),
            P("tensor"),
            P("tensor", None),
            P(),
            P(),
            P(),
            P(None, "tensor"),
            P("tensor"),
            P("tensor", None),
            P(),
        ),
        check_vma=False,
    )
```
